32 devices in a mesh: pipe: 2 (over core), ctx: 16 (over z, y, x).
Axes of the slice: x: 2, y: 2, z: 4, core: 2. Of those that a mesh axis runs over, the one named last changes fastest.
Arguments:
- states: bfloat16 [2, 2048, 2048], P('pipe', 'ctx'), may hold values from -6 to 6
- norm_gain: float32 [2, 2048], P('pipe'), may hold values from 0.25 to 1.75
- w_in: bfloat16 [2, 2048, 1536], P('pipe', 'ctx'), may hold values from -1 to 1
- w_out: bfloat16 [2, 1024, 2048], P('pipe', 'ctx'), may hold values from -0.1875 to 0.1875
- lengths: int32 [2, 4], replicated, may hold values from 1 to 1024, 2048 in all within a row
Outputs:
- moved: bfloat16 [2, 2048, 2048], P('pipe', 'ctx')
The draws below stay inside these ranges and needn't reach their ends.
Inputs may be any that keep to these rules, and one draw needn't show every extreme that they name: Each row of lengths lays the responses of one micro-batch end to end over the 2048 positions.
All inputs are finite; a program needn't handle non-finite values.
Results may differ from the reference program's by a relative error of at most 0.0045.
Values may be sent and summed in bfloat16 or wider, within the bound.
No kernel may reach another device: no remote copies, remote signals or barrier semaphores. Data moves between devices by JAX's collectives and lax.ppermute only.
A program may use at most 64 MiB of HBM per device.

```python
import math
import jax
import jax.numpy as jnp
import numpy as np
from jax import lax

D = 2048
HEAD_DIM = 64
HEADS = 16
KV_HEADS = 4
LAYERS = 2
TOKENS = 2048
QKV = 1536
RESP_MAX = 1024
DOCS = 4
N_PIPE = 2


def draw_states(key, part):
    entries = jnp.clip(jax.random.normal(jax.random.fold_in(key, 501), (LAYERS, TOKENS, D), jnp.float32), -6.0, 6.0)
    return entries.astype(jnp.bfloat16)


def draw_w_in(key, part):
    entries = jax.random.normal(jax.random.fold_in(key, 601), (LAYERS, D, QKV), jnp.float32) * D ** (-0.5)
    return jnp.clip(entries, -1.0, 1.0).astype(jnp.bfloat16)


def block_levels(stream_key, extent, pieces, low, top_value):
    factor_of = 1.0
    for dim, blocks in pieces:
        steps = jax.random.uniform(jax.random.fold_in(jax.random.fold_in(stream_key, 6), dim), (blocks,), jnp.float32, low / len(pieces), top_value / len(pieces))
        factor_of = factor_of * jnp.repeat(jnp.exp(steps), extent[dim] // blocks).reshape((-1,) + (1,) * (len(extent) - 1 - dim))
    return factor_of


def length_profile(amount, total, limit, skew):
    weights = [(1 << 20) // math.isqrt(standing ** skew) + 1 for standing in range(2, amount + 1)]
    rest, counts = total - limit - (amount - 1), [1] * (amount - 1)
    while rest > 0:
        movable = [i for i in range(amount - 1) if counts[i] < limit]
        pool, budget = sum([weights[i] for i in movable]), rest
        for i in movable:
            more = min(limit - counts[i], max(1, budget * weights[i] // pool), rest)
            counts[i] = counts[i] + more
            rest = rest - more
    return np.array([limit] + counts)


def ragged_sizes(own_key, count, total, most, skew):
    if count == 2:
        one = jax.random.randint(own_key, (), max(1, total - most), min(most, total - 1) + 1)
        return jnp.stack([one, total - one])
    tallies = jnp.asarray(length_profile(count, total, most, skew), jnp.int32)
    couples = (count - 1) // 2
    source_of, receiver = tallies[1:1 + 2 * couples:2], tallies[2:2 + 2 * couples:2]
    room = jnp.minimum(source_of - 1, most - receiver)
    passed = jax.random.randint(jax.random.fold_in(own_key, 1), (couples,), 0, 1 << 20) % (room + 1)
    tallies = tallies.at[1:1 + 2 * couples:2].set(source_of - passed).at[2:2 + 2 * couples:2].set(receiver + passed)
    return tallies[jax.random.permutation(jax.random.fold_in(own_key, 2), count)]


def noise(key, shape, deviation, limit, pieces=(), kind=jnp.bfloat16):
    level = block_levels(key, shape, pieces, -0.22, 0.18) if pieces else 1.0
    drawn = jax.random.normal(key, shape, jnp.float32) * deviation * level
    return jnp.minimum(jnp.maximum(drawn, -limit), limit).astype(kind)


def setup_inputs(seed: int = 0) -> dict:
    splits = jax.random.split(jax.random.key(seed), 6)
    states = draw_states(jax.random.fold_in(splits[5], 71), 0)
    norm_gain = jnp.clip(1.0 + 0.15 * jax.random.normal(splits[1], (LAYERS, D), jnp.float32), 0.25, 1.75)
    w_in = draw_w_in(jax.random.fold_in(splits[5], 71), 0)
    w_out = noise(splits[3], (LAYERS, HEADS * HEAD_DIM, D), (HEADS * HEAD_DIM) ** -0.5, 0.1875, ((0, 2), (1, 16)))
    lengths = jax.vmap(lambda own: ragged_sizes(own, DOCS, TOKENS, RESP_MAX, 1))(jax.random.split(splits[4], LAYERS)).reshape((LAYERS, DOCS)).astype(jnp.int32)
    return {"states": states, "norm_gain": norm_gain, "w_in": w_in, "w_out": w_out, "lengths": lengths}


epsilon = 1e-05
rope_base = 500000.0
masked_score = -1e+30

def locate(doc_lengths, spots):
    doc_ends = jnp.cumsum(doc_lengths).astype(jnp.int32)
    segment = lax.optimization_barrier(jnp.sum((doc_ends[None, :] <= spots[:, None]).astype(jnp.int32), axis=1)).astype(jnp.int32)
    starts = (doc_ends - doc_lengths).astype(jnp.int32)
    labels = jnp.arange(doc_lengths.shape[0], dtype=jnp.int32)
    first = lax.optimization_barrier(jnp.sum(jnp.where(segment[:, None] == labels[None, :], starts[None, :], 0), axis=1)).astype(jnp.int32)
    return (segment, (spots - first).astype(jnp.int32))

def rotate_pairs(heads_data, position):
    half_dim = heads_data.shape[-1] // 2
    inverse = rope_base ** (-jnp.arange(half_dim, dtype=jnp.float32) * 2.0 / heads_data.shape[-1])
    angles = position.astype(jnp.float32)[:, None] * inverse[None, :]
    cosine = jnp.cos(angles)[:, None, :]
    sine_part = jnp.sin(angles)[:, None, :]
    first_half = heads_data[..., :half_dim]
    second_half = heads_data[..., half_dim:]
    return jnp.concatenate([first_half * cosine - second_half * sine_part, second_half * cosine + first_half * sine_part], -1)

def attention_layer(inputs, gain, weight_in, weight_out, doc_lengths):
    wide = inputs.astype(jnp.float32)
    normed = (wide * lax.rsqrt(lax.optimization_barrier(jnp.mean(wide * wide, -1, keepdims=True)) + epsilon) * gain).astype(jnp.bfloat16)
    proj = jnp.dot(normed, weight_in, preferred_element_type=jnp.float32)
    q_width = HEADS * HEAD_DIM
    k_width = KV_HEADS * HEAD_DIM
    spots = jnp.arange(TOKENS, dtype=jnp.int32)
    segment, position = locate(doc_lengths, spots)
    queries = rotate_pairs(proj[:, :q_width].reshape(TOKENS, HEADS, HEAD_DIM), position).astype(jnp.bfloat16)
    keys_rot = rotate_pairs(proj[:, q_width:q_width + k_width].reshape(TOKENS, KV_HEADS, HEAD_DIM), position).astype(jnp.bfloat16)
    values = proj[:, q_width + k_width:].reshape(TOKENS, KV_HEADS, HEAD_DIM).astype(jnp.bfloat16)
    group = HEADS // KV_HEADS
    keys_wide = keys_rot.astype(jnp.float32)
    values_wide = values.astype(jnp.float32)
    block_rows = math.gcd(TOKENS, 512)

    def query_block(block_idx):
        first_row = block_idx * block_rows
        query_part = lax.dynamic_slice_in_dim(queries, first_row, block_rows, 0).astype(jnp.float32)
        query_part = query_part.reshape(block_rows, KV_HEADS, group, HEAD_DIM)
        scores = jnp.einsum('tgjd,rgd->gjtr', query_part, keys_wide) * HEAD_DIM ** (-0.5)
        query_spots = first_row + jnp.arange(block_rows, dtype=jnp.int32)
        query_seg = lax.dynamic_slice_in_dim(segment, first_row, block_rows, 0)
        allowed = (query_seg[:, None] == segment[None, :]) & (spots[None, :] <= query_spots[:, None])
        scores = jnp.where(allowed, scores, masked_score)
        row_max = lax.optimization_barrier(jnp.max(scores, -1, keepdims=True))
        probs = jnp.where(allowed, jnp.exp(scores - row_max), 0.0)
        denom = lax.optimization_barrier(jnp.sum(probs, -1))
        rounded = probs.astype(jnp.bfloat16).astype(jnp.float32)
        attended = jnp.einsum('gjtr,rgd->gjtd', rounded, values_wide) / denom[..., None]
        return attended.transpose(2, 0, 1, 3).reshape(block_rows, HEADS * HEAD_DIM).astype(jnp.bfloat16)
    attended = lax.map(query_block, jnp.arange(TOKENS // block_rows, dtype=jnp.int32))
    attended = attended.reshape(TOKENS, HEADS * HEAD_DIM)
    output = jnp.dot(attended, weight_out, preferred_element_type=jnp.float32)
    return (wide + output).astype(jnp.bfloat16)

def reference(states, norm_gain, w_in, w_out, lengths):
    results = []
    for section_index in range(N_PIPE):
        results.append(attention_layer(states[section_index], norm_gain[section_index], w_in[section_index], w_out[section_index], lengths[section_index]))
    return jnp.stack([results[(section_index - 1) % N_PIPE] for section_index in range(N_PIPE)])
```

```python
import functools

import jax
import jax.numpy as jnp
from jax import lax
from jax.experimental import pallas as pl
from jax.experimental.pallas import tpu as pltpu
from jax.sharding import PartitionSpec as P

HEAD_DIM = 64
HEADS = 16
KV_HEADS = 4
GROUP = HEADS // KV_HEADS

epsilon = 1e-05
rope_base = 500000.0
masked_score = -1e30
KEY_BLOCK = 256

VMEM = pltpu.MemorySpace.VMEM
SMEM = pltpu.MemorySpace.SMEM


def call(kernel, out_shape, scratch=(), flops=0, moved=0):
    def run(scalars, *arrays):
        return pl.pallas_call(
            kernel,
            out_shape=out_shape,
            in_specs=[pl.BlockSpec(memory_space=SMEM)]
            + [pl.BlockSpec(memory_space=VMEM)] * len(arrays),
            out_specs=jax.tree.map(lambda _: pl.BlockSpec(memory_space=VMEM), out_shape),
            scratch_shapes=list(scratch),
            cost_estimate=pl.CostEstimate(flops=flops, bytes_accessed=moved, transcendentals=0),
        )(scalars, *arrays)

    return run


def stack_kernel(s_ref, b0, b1, b2, b3, out_ref):
    size = b0.shape[0]
    for k, ref in enumerate((b0, b1, b2, b3)):
        at = pl.multiple_of(lax.bitwise_xor(s_ref[1], k) * size, 16)
        out_ref[pl.ds(at, size), :] = ref[...]


def norm_kernel(s_ref, x0, x1, x2, x3a, x3b, gain_ref, normed_ref, rest_ref):
    col = s_ref[1]
    rows = x0.shape[0]
    tile = rest_ref.shape[1]

    def one(ref, first, count, place):
        wide = ref[...].astype(jnp.float32)
        scale = lax.rsqrt(jnp.mean(wide * wide, -1, keepdims=True) + epsilon)
        at = pl.ds(pl.multiple_of(place * rows + first, 8), count)
        normed_ref[at, :] = (wide * scale * gain_ref[...]).astype(jnp.bfloat16)
        rest_ref[at, :] = ref[:, pl.ds(pl.multiple_of(col * tile, 128), tile)]

    half = rows // 2
    one(x0, 0, rows, col)
    one(x1, 0, rows, lax.bitwise_xor(col, 1))
    one(x2, 0, rows, lax.bitwise_xor(col, 2))
    one(x3a, 0, half, lax.bitwise_xor(col, 3))
    one(x3b, half, half, lax.bitwise_xor(col, 3))


def rotated(part, cosine, sine):
    lane = lax.broadcasted_iota(jnp.int32, part.shape, 1)
    half = HEAD_DIM // 2
    ahead = pltpu.roll(part, 128 - half, 1)
    behind = pltpu.roll(part, half, 1)
    other = jnp.where(lax.rem(lane, HEAD_DIM) < half, ahead, behind)
    return part * cosine + other * sine


def qkv_kernel(count, s_ref, normed_ref, cos_ref, sin_ref, *refs):
    blocks, (q_ref, kv_ref) = refs[:count], refs[count:]
    deep = blocks[0].shape[0]
    proj = None
    for d in range(count):
        cols = pl.ds(pl.multiple_of(s_ref[8 + d] * deep, 128), deep)
        term = jnp.dot(normed_ref[:, cols], blocks[d][...], preferred_element_type=jnp.float32)
        proj = term if proj is None else proj + term
    cosine, sine = cos_ref[...], sin_ref[...]
    wide = GROUP * HEAD_DIM
    for g in range(wide // 128):
        part = rotated(proj[:, g * 128 : (g + 1) * 128], cosine, sine)
        q_ref[:, g * 128 : (g + 1) * 128] = (part * HEAD_DIM ** (-0.5)).astype(jnp.bfloat16)
    part = proj[:, wide : wide + 128]
    lane = lax.broadcasted_iota(jnp.int32, part.shape, 1)
    kv_ref[...] = jnp.where(lane < HEAD_DIM, rotated(part, cosine, sine), part).astype(jnp.bfloat16)


def attention_kernel(docs, reach, s_ref, q_ref, *refs):
    kv_refs = refs[: reach + 1]
    out_ref, kv_all, scores, top, total, accum = refs[reach + 1 :]
    span, tile = q_ref.shape[0], 128
    base = (s_ref[0] - reach) * span
    for r in range(reach + 1):
        kv_all[r * span : (r + 1) * span, :] = kv_refs[r][...]

    def doc_start(spots):
        ends, start = 0, spots * 0
        for d in range(docs):
            long = s_ref[32 + d]
            ends = ends + long
            start = start + jnp.where(spots >= ends, long, 0)
        return start

    @pl.loop(0, span // tile)
    def _(i):
        first = s_ref[0] * span + i * tile
        rows = pl.ds(pl.multiple_of(i * tile, tile), tile)
        low = lax.max(doc_start(first) - base, 0) // KEY_BLOCK
        high = (first + tile - 1 - base) // KEY_BLOCK + 1
        flat = q_ref[rows, :]
        blank = jnp.zeros((tile, 128 - HEAD_DIM), jnp.bfloat16)
        stacked = jnp.concatenate(
            [
                jnp.concatenate([flat[:, h * HEAD_DIM : (h + 1) * HEAD_DIM], blank], 1)
                for h in range(GROUP)
            ],
            0,
        )
        spots = first + lax.broadcasted_iota(jnp.int32, (tile, 1), 0)
        starts = doc_start(spots)
        top[...] = jnp.full(top.shape, masked_score, jnp.float32)

        @pl.loop(low, high)
        def _(j):
            keys = kv_all[pl.ds(pl.multiple_of(j * KEY_BLOCK, KEY_BLOCK), KEY_BLOCK), :]
            part = lax.dot_general(
                stacked, keys, (((1,), (1,)), ((), ())), preferred_element_type=jnp.float32
            )
            key_spots = (
                base + j * KEY_BLOCK + lax.broadcasted_iota(jnp.int32, (tile, KEY_BLOCK), 1)
            )
            allowed = (key_spots <= spots) & (key_spots >= starts)
            for h in range(GROUP):
                at = slice(h * tile, (h + 1) * tile)
                kept = jnp.where(allowed, part[at], masked_score)
                scores[j, at, :] = kept
                best = top[at, :]
                for k in range(KEY_BLOCK // 128):
                    best = jnp.maximum(best, kept[:, k * 128 : (k + 1) * 128])
                top[at, :] = best

        highest = jnp.max(top[...], -1, keepdims=True)
        total[...] = jnp.zeros(total.shape, jnp.float32)
        accum[...] = jnp.zeros(accum.shape, jnp.float32)

        @pl.loop(low, high)
        def _(j):
            probs = jnp.exp(scores[j] - highest)
            added = total[...]
            for k in range(KEY_BLOCK // 128):
                added = added + probs[:, k * 128 : (k + 1) * 128]
            total[...] = added
            both = kv_all[pl.ds(pl.multiple_of(j * KEY_BLOCK, KEY_BLOCK), KEY_BLOCK), :]
            accum[...] += jnp.dot(
                probs.astype(jnp.bfloat16), both, preferred_element_type=jnp.float32
            )

        done = accum[...] / jnp.sum(total[...], -1, keepdims=True)
        out_ref[rows, :] = jnp.concatenate(
            [done[h * tile : (h + 1) * tile, HEAD_DIM : 2 * HEAD_DIM] for h in range(GROUP)], 1
        ).astype(jnp.bfloat16)


def output_kernel(count, s_ref, a0, a1, a2, a3a, a3b, rest_ref, *refs):
    blocks = refs[:count]
    outs = refs[count : count + KV_HEADS]
    weight = refs[count + KV_HEADS]
    col = s_ref[1]
    deep = blocks[0].shape[0]
    span, each = a0.shape
    for d in range(count):
        row = pl.multiple_of(s_ref[8 + d] * deep, 128)
        weight[pl.ds(row, deep), :] = blocks[d][...]

    def rows_of(k):
        place = lax.bitwise_xor(col, k) * each
        return weight[pl.ds(pl.multiple_of(place, 128), each), :]

    w0, w1, w2, w3 = rows_of(0), rows_of(1), rows_of(2), rows_of(3)
    size = span // KV_HEADS
    for k in range(KV_HEADS):
        token = lax.bitwise_xor(col, k)
        at = pl.ds(pl.multiple_of(token * size, size), size)
        later = token >= KV_HEADS // 2
        there = pl.ds(pl.multiple_of(lax.rem(token, KV_HEADS // 2) * size, size), size)
        third = jnp.where(later, a3b[there, :], a3a[there, :])
        value = jnp.dot(a0[at, :], w0, preferred_element_type=jnp.float32)
        value += jnp.dot(a1[at, :], w1, preferred_element_type=jnp.float32)
        value += jnp.dot(a2[at, :], w2, preferred_element_type=jnp.float32)
        value += jnp.dot(third, w3, preferred_element_type=jnp.float32)
        outs[k][...] = (rest_ref[at, :].astype(jnp.float32) + value).astype(jnp.bfloat16)


def place_kernel(s_ref, r0, r1, r2, r3, out_ref):
    width = r0.shape[1]
    for k, ref in enumerate((r0, r1, r2, r3)):
        at = pl.multiple_of(lax.bitwise_xor(s_ref[1], k) * width, 128)
        out_ref[:, pl.ds(at, width)] = ref[...]


def doc_starts(doc_lengths, spots):
    ends = jnp.cumsum(doc_lengths)
    return jnp.sum(jnp.where(ends[None, :] <= spots[:, None], doc_lengths[None, :], 0), axis=1)


def body(states, norm_gain, w_in, w_out, lengths):
    section = lax.axis_index("pipe")
    sections = lax.axis_size("pipe")
    me = lax.axis_index("ctx")
    count = lax.axis_size("ctx")
    planes = count // KV_HEADS
    col = lax.rem(me, KV_HEADS)
    plane = me // KV_HEADS
    x = states[0]
    rows, width = x.shape
    span = rows * KV_HEADS
    tile = width // KV_HEADS
    q_width, k_width = HEADS * HEAD_DIM, KV_HEADS * HEAD_DIM
    each = GROUP * HEAD_DIM

    order = list(range(0, planes, 2)) + list(range(1, planes, 2))[::-1]
    ring = [
        (order[i] * KV_HEADS + c, order[(i + 1) % planes] * KV_HEADS + c)
        for i in range(planes)
        for c in range(KV_HEADS)
    ]

    def across(value, k):
        return lax.ppermute(value, "ctx", [(i, i ^ k) for i in range(count)])

    def exchanged(blocks):
        own = lax.dynamic_index_in_dim(blocks, col, 0, keepdims=False)
        got = [
            across(lax.dynamic_index_in_dim(blocks, lax.bitwise_xor(col, k), 0, keepdims=False), k)
            for k in range(1, KV_HEADS)
        ]
        size, wide = own.shape
        shape = jax.ShapeDtypeStruct((KV_HEADS * size, wide), own.dtype)
        return call(stack_kernel, shape, moved=4 * KV_HEADS * size * wide)(scalars, own, *got)

    def ringed(block):
        held = [block]
        for _ in range(planes - 1):
            held.append(lax.ppermute(held[-1], "ctx", ring))
        return held

    def gathered(value):
        half = value.shape[0] // 2
        one, two = across(value, 1), across(value, 2)
        return [value, one, two, across(one[:half], 2), across(two[half:], 1)]

    doc_lengths = lax.dynamic_index_in_dim(lengths, section, 0, keepdims=False)
    docs = doc_lengths.shape[0]
    place_in_ring = jnp.zeros((), jnp.int32)
    for i, p in enumerate(order):
        place_in_ring = jnp.where(plane == p, i, place_in_ring)
    steps = lax.rem(place_in_ring - jnp.arange(planes, dtype=jnp.int32) + planes, planes)
    holders = jnp.where(2 * steps < planes + planes % 2, 2 * steps, 2 * (planes - 1 - steps) + 1)
    scalars = jnp.zeros((64,), jnp.int32)
    scalars = scalars.at[0].set(plane).at[1].set(col)
    scalars = scalars.at[8 : 8 + planes].set(holders).at[32 : 32 + docs].set(doc_lengths)

    w = w_in[0]
    by_col = jnp.concatenate(
        [
            w[:, :q_width].reshape(-1, KV_HEADS, each),
            w[:, q_width : q_width + k_width].reshape(-1, KV_HEADS, HEAD_DIM),
            w[:, q_width + k_width :].reshape(-1, KV_HEADS, HEAD_DIM),
        ],
        2,
    ).transpose(1, 0, 2)
    in_blocks = ringed(exchanged(by_col))
    out_by_col = w_out[0].reshape(-1, KV_HEADS, tile).transpose(1, 0, 2)

    parts = gathered(x)
    normed, rest = call(
        norm_kernel,
        (
            jax.ShapeDtypeStruct((span, width), jnp.bfloat16),
            jax.ShapeDtypeStruct((span, tile), jnp.bfloat16),
        ),
        moved=4 * span * width,
    )(scalars, *parts, norm_gain)

    spots = plane * span + jnp.arange(span, dtype=jnp.int32)
    position = (spots - doc_starts(doc_lengths, spots)).astype(jnp.float32)
    half = HEAD_DIM // 2
    inverse = rope_base ** (-jnp.arange(half, dtype=jnp.float32) * 2.0 / HEAD_DIM)
    angles = position[:, None] * inverse[None, :]
    cosine = jnp.tile(jnp.cos(angles), (1, 128 // half))
    sine = jnp.sin(angles)
    sine = jnp.tile(jnp.concatenate([-sine, sine], 1), (1, 128 // HEAD_DIM))

    queries, keys_values = call(
        functools.partial(qkv_kernel, planes),
        (
            jax.ShapeDtypeStruct((span, each), jnp.bfloat16),
            jax.ShapeDtypeStruct((span, 2 * HEAD_DIM), jnp.bfloat16),
        ),
        flops=2 * span * width * (each + 2 * HEAD_DIM),
        moved=2 * span * width + 2 * width * (each + 2 * HEAD_DIM),
    )(scalars, normed, cosine, sine, *in_blocks)

    longest = min(1024, 8 * rows, rows * count // 2)
    reach = min(planes - 1, (longest + span - 2) // span)
    history = [keys_values]
    for r in range(1, reach + 1):
        pairs = [(i, i + r * KV_HEADS) for i in range(count - r * KV_HEADS)]
        history.insert(0, lax.ppermute(keys_values, "ctx", pairs))

    out_blocks = ringed(exchanged(out_by_col))

    key_blocks = (reach + 1) * span // KEY_BLOCK
    attended = call(
        functools.partial(attention_kernel, docs, reach),
        jax.ShapeDtypeStruct((span, each), jnp.bfloat16),
        scratch=[
            pltpu.VMEM(((reach + 1) * span, 2 * HEAD_DIM), jnp.bfloat16),
            pltpu.VMEM((key_blocks, GROUP * 128, KEY_BLOCK), jnp.float32),
            pltpu.VMEM((GROUP * 128, 128), jnp.float32),
            pltpu.VMEM((GROUP * 128, 128), jnp.float32),
            pltpu.VMEM((GROUP * 128, 2 * HEAD_DIM), jnp.float32),
        ],
        flops=8 * span * each * span,
        moved=4 * span * each,
    )(scalars, queries, *history)

    results = call(
        functools.partial(output_kernel, planes),
        (jax.ShapeDtypeStruct((rows, tile), jnp.bfloat16),) * KV_HEADS,
        scratch=[pltpu.VMEM((q_width, tile), jnp.bfloat16)],
        flops=2 * span * q_width * tile,
        moved=2 * q_width * tile + 4 * span * tile,
    )(scalars, *gathered(attended), rest, *out_blocks)

    landed = []
    for k in range(KV_HEADS):
        pairs = [
            (s * count + i, (s + 1) % sections * count + (i ^ k))
            for s in range(sections)
            for i in range(count)
        ]
        landed.append(lax.ppermute(results[k], ("pipe", "ctx"), pairs))
    moved = call(place_kernel, jax.ShapeDtypeStruct((rows, width), jnp.bfloat16), moved=4 * rows * width)(
        scalars, *landed
    )
    return moved[None]


def solution(mesh):
    return jax.shard_map(
        body,
        mesh=mesh,
        in_specs=(
            P("pipe", "ctx", None),
            P("pipe", None),
            P("pipe", "ctx", None),
            P("pipe", "ctx", None),
            P(),
        ),
        out_specs=P("pipe", "ctx", None),
        check_vma=False,
    )
```

```python
import functools

import jax
import jax.numpy as jnp
from jax import lax
from jax.experimental import pallas as pl
from jax.experimental.pallas import tpu as pltpu
from jax.sharding import PartitionSpec as P

HEAD_DIM = 64
HEADS = 16
KV_HEADS = 4
GROUP = HEADS // KV_HEADS

epsilon = 1e-05
rope_base = 500000.0
masked_score = -1e30
KEY_BLOCK = 256

VMEM = pltpu.MemorySpace.VMEM
SMEM = pltpu.MemorySpace.SMEM


def call(kernel, out_shape, scratch=(), flops=0, moved=0):
    def run(scalars, *arrays):
        return pl.pallas_call(
            kernel,
            out_shape=jax.tree.map(lambda o: VMEM(o.shape, o.dtype), out_shape),
            in_specs=[pl.BlockSpec(memory_space=SMEM)]
            + [pl.BlockSpec(memory_space=VMEM)] * len(arrays),
            out_specs=jax.tree.map(lambda _: pl.BlockSpec(memory_space=VMEM), out_shape),
            scratch_shapes=list(scratch),
            compiler_params=pltpu.CompilerParams(vmem_limit_bytes=16 << 20),
            cost_estimate=pl.CostEstimate(flops=flops, bytes_accessed=moved, transcendentals=0),
        )(scalars, *[pltpu.with_memory_space_constraint(a, VMEM) for a in arrays])

    return run


def stack_kernel(s_ref, b0, b1, b2, b3, out_ref):
    size = b0.shape[0]
    for k, ref in enumerate((b0, b1, b2, b3)):
        at = pl.multiple_of(lax.bitwise_xor(s_ref[1], k) * size, 16)
        out_ref[pl.ds(at, size), :] = ref[...]


def norm_kernel(s_ref, x0, x1, x2, x3a, x3b, gain_ref, normed_ref, rest_ref):
    col = s_ref[1]
    rows = x0.shape[0]
    tile = rest_ref.shape[1]

    def one(ref, first, count, place):
        wide = ref[...].astype(jnp.float32)
        scale = lax.rsqrt(jnp.mean(wide * wide, -1, keepdims=True) + epsilon)
        at = pl.ds(pl.multiple_of(place * rows + first, 8), count)
        normed_ref[at, :] = (wide * scale * gain_ref[...]).astype(jnp.bfloat16)
        rest_ref[at, :] = ref[:, pl.ds(pl.multiple_of(col * tile, 128), tile)]

    half = rows // 2
    one(x0, 0, rows, col)
    one(x1, 0, rows, lax.bitwise_xor(col, 1))
    one(x2, 0, rows, lax.bitwise_xor(col, 2))
    one(x3a, 0, half, lax.bitwise_xor(col, 3))
    one(x3b, half, half, lax.bitwise_xor(col, 3))


def rotated(part, cosine, sine):
    lane = lax.broadcasted_iota(jnp.int32, part.shape, 1)
    half = HEAD_DIM // 2
    ahead = pltpu.roll(part, 128 - half, 1)
    behind = pltpu.roll(part, half, 1)
    other = jnp.where(lax.rem(lane, HEAD_DIM) < half, ahead, behind)
    return part * cosine + other * sine


def qkv_kernel(count, s_ref, normed_ref, cos_ref, sin_ref, *refs):
    blocks, (q_ref, kv_ref) = refs[:count], refs[count:]
    deep = blocks[0].shape[0]
    proj = None
    for d in range(count):
        cols = pl.ds(pl.multiple_of(s_ref[8 + d] * deep, 128), deep)
        term = jnp.dot(normed_ref[:, cols], blocks[d][...], preferred_element_type=jnp.float32)
        proj = term if proj is None else proj + term
    cosine, sine = cos_ref[...], sin_ref[...]
    wide = GROUP * HEAD_DIM
    for g in range(wide // 128):
        part = rotated(proj[:, g * 128 : (g + 1) * 128], cosine, sine)
        q_ref[:, g * 128 : (g + 1) * 128] = (part * HEAD_DIM ** (-0.5)).astype(jnp.bfloat16)
    part = proj[:, wide : wide + 128]
    lane = lax.broadcasted_iota(jnp.int32, part.shape, 1)
    kv_ref[...] = jnp.where(lane < HEAD_DIM, rotated(part, cosine, sine), part).astype(jnp.bfloat16)


def attention_kernel(docs, reach, s_ref, q_ref, *refs):
    kv_refs = refs[: reach + 1]
    out_ref, kv_all, scores, top, total, accum = refs[reach + 1 :]
    span, tile = q_ref.shape[0], 128
    base = (s_ref[0] - reach) * span
    for r in range(reach + 1):
        kv_all[r * span : (r + 1) * span, :] = kv_refs[r][...]

    def doc_start(spots):
        ends, start = 0, spots * 0
        for d in range(docs):
            long = s_ref[32 + d]
            ends = ends + long
            start = start + jnp.where(spots >= ends, long, 0)
        return start

    @pl.loop(0, span // tile)
    def _(i):
        first = s_ref[0] * span + i * tile
        rows = pl.ds(pl.multiple_of(i * tile, tile), tile)
        low = lax.max(doc_start(first) - base, 0) // KEY_BLOCK
        high = (first + tile - 1 - base) // KEY_BLOCK + 1
        flat = q_ref[rows, :]
        blank = jnp.zeros((tile, 128 - HEAD_DIM), jnp.bfloat16)
        stacked = jnp.concatenate(
            [
                jnp.concatenate([flat[:, h * HEAD_DIM : (h + 1) * HEAD_DIM], blank], 1)
                for h in range(GROUP)
            ],
            0,
        )
        spots = first + lax.broadcasted_iota(jnp.int32, (tile, 1), 0)
        starts = doc_start(spots)
        top[...] = jnp.full(top.shape, masked_score, jnp.float32)

        @pl.loop(low, high)
        def _(j):
            keys = kv_all[pl.ds(pl.multiple_of(j * KEY_BLOCK, KEY_BLOCK), KEY_BLOCK), :]
            part = lax.dot_general(
                stacked, keys, (((1,), (1,)), ((), ())), preferred_element_type=jnp.float32
            )
            key_spots = (
                base + j * KEY_BLOCK + lax.broadcasted_iota(jnp.int32, (tile, KEY_BLOCK), 1)
            )
            allowed = (key_spots <= spots) & (key_spots >= starts)
            for h in range(GROUP):
                at = slice(h * tile, (h + 1) * tile)
                kept = jnp.where(allowed, part[at], masked_score)
                scores[j, at, :] = kept
                best = top[at, :]
                for k in range(KEY_BLOCK // 128):
                    best = jnp.maximum(best, kept[:, k * 128 : (k + 1) * 128])
                top[at, :] = best

        highest = jnp.max(top[...], -1, keepdims=True)
        total[...] = jnp.zeros(total.shape, jnp.float32)
        accum[...] = jnp.zeros(accum.shape, jnp.float32)

        @pl.loop(low, high)
        def _(j):
            probs = jnp.exp(scores[j] - highest)
            added = total[...]
            for k in range(KEY_BLOCK // 128):
                added = added + probs[:, k * 128 : (k + 1) * 128]
            total[...] = added
            both = kv_all[pl.ds(pl.multiple_of(j * KEY_BLOCK, KEY_BLOCK), KEY_BLOCK), :]
            accum[...] += jnp.dot(
                probs.astype(jnp.bfloat16), both, preferred_element_type=jnp.float32
            )

        done = accum[...] / jnp.sum(total[...], -1, keepdims=True)
        out_ref[rows, :] = jnp.concatenate(
            [done[h * tile : (h + 1) * tile, HEAD_DIM : 2 * HEAD_DIM] for h in range(GROUP)], 1
        ).astype(jnp.bfloat16)


def output_kernel(count, s_ref, a0, a1, a2, a3a, a3b, rest_ref, *refs):
    blocks = refs[:count]
    outs = refs[count : count + KV_HEADS]
    weight = refs[count + KV_HEADS]
    col = s_ref[1]
    deep = blocks[0].shape[0]
    span, each = a0.shape
    for d in range(count):
        row = pl.multiple_of(s_ref[8 + d] * deep, 128)
        weight[pl.ds(row, deep), :] = blocks[d][...]

    def rows_of(k):
        place = lax.bitwise_xor(col, k) * each
        return weight[pl.ds(pl.multiple_of(place, 128), each), :]

    w0, w1, w2, w3 = rows_of(0), rows_of(1), rows_of(2), rows_of(3)
    size = span // KV_HEADS
    for k in range(KV_HEADS):
        token = lax.bitwise_xor(col, k)
        at = pl.ds(pl.multiple_of(token * size, size), size)
        later = token >= KV_HEADS // 2
        there = pl.ds(pl.multiple_of(lax.rem(token, KV_HEADS // 2) * size, size), size)
        third = jnp.where(later, a3b[there, :], a3a[there, :])
        value = jnp.dot(a0[at, :], w0, preferred_element_type=jnp.float32)
        value += jnp.dot(a1[at, :], w1, preferred_element_type=jnp.float32)
        value += jnp.dot(a2[at, :], w2, preferred_element_type=jnp.float32)
        value += jnp.dot(third, w3, preferred_element_type=jnp.float32)
        outs[k][...] = (rest_ref[at, :].astype(jnp.float32) + value).astype(jnp.bfloat16)


def place_kernel(s_ref, r0, r1, r2, r3, out_ref):
    width = r0.shape[1]
    for k, ref in enumerate((r0, r1, r2, r3)):
        at = pl.multiple_of(lax.bitwise_xor(s_ref[1], k) * width, 128)
        out_ref[:, pl.ds(at, width)] = ref[...]


def doc_starts(doc_lengths, spots):
    ends = jnp.cumsum(doc_lengths)
    return jnp.sum(jnp.where(ends[None, :] <= spots[:, None], doc_lengths[None, :], 0), axis=1)


def body(states, norm_gain, w_in, w_out, lengths):
    section = lax.axis_index("pipe")
    sections = lax.axis_size("pipe")
    me = lax.axis_index("ctx")
    count = lax.axis_size("ctx")
    planes = count // KV_HEADS
    col = lax.rem(me, KV_HEADS)
    plane = me // KV_HEADS
    x = states[0]
    rows, width = x.shape
    span = rows * KV_HEADS
    tile = width // KV_HEADS
    q_width, k_width = HEADS * HEAD_DIM, KV_HEADS * HEAD_DIM
    each = GROUP * HEAD_DIM

    order = list(range(0, planes, 2)) + list(range(1, planes, 2))[::-1]
    ring = [
        (order[i] * KV_HEADS + c, order[(i + 1) % planes] * KV_HEADS + c)
        for i in range(planes)
        for c in range(KV_HEADS)
    ]

    def across(value, k):
        return lax.ppermute(value, "ctx", [(i, i ^ k) for i in range(count)])

    def exchanged(blocks):
        own = lax.dynamic_index_in_dim(blocks, col, 0, keepdims=False)
        got = [
            across(lax.dynamic_index_in_dim(blocks, lax.bitwise_xor(col, k), 0, keepdims=False), k)
            for k in range(1, KV_HEADS)
        ]
        size, wide = own.shape
        shape = jax.ShapeDtypeStruct((KV_HEADS * size, wide), own.dtype)
        return call(stack_kernel, shape, moved=4 * KV_HEADS * size * wide)(scalars, own, *got)

    def ringed(block):
        held = [block]
        for _ in range(planes - 1):
            held.append(lax.ppermute(held[-1], "ctx", ring))
        return held

    def gathered(value):
        half = value.shape[0] // 2
        one, two = across(value, 1), across(value, 2)
        return [value, one, two, across(one[:half], 2), across(two[half:], 1)]

    doc_lengths = lax.dynamic_index_in_dim(lengths, section, 0, keepdims=False)
    docs = doc_lengths.shape[0]
    place_in_ring = jnp.zeros((), jnp.int32)
    for i, p in enumerate(order):
        place_in_ring = jnp.where(plane == p, i, place_in_ring)
    steps = lax.rem(place_in_ring - jnp.arange(planes, dtype=jnp.int32) + planes, planes)
    holders = jnp.where(2 * steps < planes + planes % 2, 2 * steps, 2 * (planes - 1 - steps) + 1)
    scalars = jnp.zeros((64,), jnp.int32)
    scalars = scalars.at[0].set(plane).at[1].set(col)
    scalars = scalars.at[8 : 8 + planes].set(holders).at[32 : 32 + docs].set(doc_lengths)

    w = w_in[0]
    by_col = jnp.concatenate(
        [
            w[:, :q_width].reshape(-1, KV_HEADS, each),
            w[:, q_width : q_width + k_width].reshape(-1, KV_HEADS, HEAD_DIM),
            w[:, q_width + k_width :].reshape(-1, KV_HEADS, HEAD_DIM),
        ],
        2,
    ).transpose(1, 0, 2)
    in_blocks = ringed(exchanged(by_col))
    out_by_col = w_out[0].reshape(-1, KV_HEADS, tile).transpose(1, 0, 2)

    parts = gathered(x)
    normed, rest = call(
        norm_kernel,
        (
            jax.ShapeDtypeStruct((span, width), jnp.bfloat16),
            jax.ShapeDtypeStruct((span, tile), jnp.bfloat16),
        ),
        moved=4 * span * width,
    )(scalars, *parts, norm_gain)

    spots = plane * span + jnp.arange(span, dtype=jnp.int32)
    position = (spots - doc_starts(doc_lengths, spots)).astype(jnp.float32)
    half = HEAD_DIM // 2
    inverse = rope_base ** (-jnp.arange(half, dtype=jnp.float32) * 2.0 / HEAD_DIM)
    angles = position[:, None] * inverse[None, :]
    cosine = jnp.tile(jnp.cos(angles), (1, 128 // half))
    sine = jnp.sin(angles)
    sine = jnp.tile(jnp.concatenate([-sine, sine], 1), (1, 128 // HEAD_DIM))

    queries, keys_values = call(
        functools.partial(qkv_kernel, planes),
        (
            jax.ShapeDtypeStruct((span, each), jnp.bfloat16),
            jax.ShapeDtypeStruct((span, 2 * HEAD_DIM), jnp.bfloat16),
        ),
        flops=2 * span * width * (each + 2 * HEAD_DIM),
        moved=2 * span * width + 2 * width * (each + 2 * HEAD_DIM),
    )(scalars, normed, cosine, sine, *in_blocks)

    longest = min(1024, 8 * rows, rows * count // 2)
    reach = min(planes - 1, (longest + span - 2) // span)
    history = [keys_values]
    for r in range(1, reach + 1):
        pairs = [(i, i + r * KV_HEADS) for i in range(count - r * KV_HEADS)]
        history.insert(0, lax.ppermute(keys_values, "ctx", pairs))

    out_blocks = ringed(exchanged(out_by_col))

    key_blocks = (reach + 1) * span // KEY_BLOCK
    attended = call(
        functools.partial(attention_kernel, docs, reach),
        jax.ShapeDtypeStruct((span, each), jnp.bfloat16),
        scratch=[
            pltpu.VMEM(((reach + 1) * span, 2 * HEAD_DIM), jnp.bfloat16),
            pltpu.VMEM((key_blocks, GROUP * 128, KEY_BLOCK), jnp.float32),
            pltpu.VMEM((GROUP * 128, 128), jnp.float32),
            pltpu.VMEM((GROUP * 128, 128), jnp.float32),
            pltpu.VMEM((GROUP * 128, 2 * HEAD_DIM), jnp.float32),
        ],
        flops=8 * span * each * span,
        moved=4 * span * each,
    )(scalars, queries, *history)

    results = call(
        functools.partial(output_kernel, planes),
        (jax.ShapeDtypeStruct((rows, tile), jnp.bfloat16),) * KV_HEADS,
        scratch=[pltpu.VMEM((q_width, tile), jnp.bfloat16)],
        flops=2 * span * q_width * tile,
        moved=2 * q_width * tile + 4 * span * tile,
    )(scalars, *gathered(attended), rest, *out_blocks)

    landed = []
    for k in range(KV_HEADS):
        pairs = [
            (s * count + i, (s + 1) % sections * count + (i ^ k))
            for s in range(sections)
            for i in range(count)
        ]
        landed.append(lax.ppermute(results[k], ("pipe", "ctx"), pairs))
    moved = call(place_kernel, jax.ShapeDtypeStruct((rows, width), jnp.bfloat16), moved=4 * rows * width)(
        scalars, *landed
    )
    return moved[None]


def solution(mesh):
    return jax.shard_map(
        body,
        mesh=mesh,
        in_specs=(
            P("pipe", "ctx", None),
            P("pipe", None),
            P("pipe", "ctx", None),
            P("pipe", "ctx", None),
            P(),
        ),
        out_specs=P("pipe", "ctx", None),
        check_vma=False,
    )
```
